32 devices in a mesh: dp: 4 (over y, x), store: 8 (over z, core).
Axes of the slice: x: 2, y: 2, z: 4, core: 2. Of those that a mesh axis runs over, the one named last changes fastest.
Arguments:
- inputs: bfloat16 [4096, 1024], P(('dp', 'store')), may hold values from -6 to 6
- lengths: int32 [32], P(('dp', 'store')), may hold values from 64 to 128, as said below
- targets: int32 [4096], P('dp'), may hold values from 0 to 34303
- attn_qkv: bfloat16 [3, 1024, 1024], replicated, may hold values from -0.1875 to 0.1875
- attn_out: bfloat16 [1024, 1024], replicated, may hold values from -1 to 1
- ffn_up: bfloat16 [1024, 4096], replicated, may hold values from -0.1875 to 0.1875
- ffn_down: bfloat16 [4096, 1024], replicated, may hold values from -0.09375 to 0.09375
- norm_gains: float32 [3, 1024], replicated, may hold values from 0.25 to 1.75
- norm_shifts: float32 [3, 1024], replicated, may hold values from -1.5 to 1.5
- biases: float32 [4, 1024], replicated, may hold values from -1.5 to 1.5
- up_bias: float32 [4096], replicated, may hold values from -1.5 to 1.5
- cluster_proj: bfloat16 [1024, 2], replicated, may hold values from -0.1875 to 0.1875
- proj_first: bfloat16 [1024, 256], replicated, may hold values from -0.1875 to 0.1875
- proj_second: bfloat16 [1024, 64], replicated, may hold values from -0.1875 to 0.1875
- head_words: bfloat16 [1024, 2560], P(None, 'store'), may hold values from -0.1875 to 0.1875
- tail_first: bfloat16 [256, 5120], P(None, 'store'), may hold values from -0.375 to 0.375
- tail_second: bfloat16 [64, 26624], P(None, 'store'), may hold values from -0.75 to 0.75
- store_keys: bfloat16 [32768, 1024], P('store'), may hold values from -6 to 6
- block_rows: int32 [4, 8, 8, 128], P('dp', 'store'), may hold values from 0 to 4095
- near_slots: int32 [4, 8, 128, 8, 16], P('dp', 'store'), may hold values from 0 to 127, as said below
- near_words: int32 [4096, 128], P(('dp', 'store')), may hold values from 0 to 32703
Outputs:
- token_loss: float32 [4096], P(('dp', 'store'))
- input_grad: float32 [4096, 1024], P(('dp', 'store'))
- qkv_grad: float32 [3, 1024, 1024], P(None, 'store')
- out_grad: float32 [1024, 1024], P('store')
- up_grad: float32 [1024, 4096], P('store')
- down_grad: float32 [4096, 1024], P('store')
- gains_grad: float32 [3, 1024], P(None, 'store')
- shifts_grad: float32 [3, 1024], P(None, 'store')
- biases_grad: float32 [4, 1024], P(None, 'store')
- up_bias_grad: float32 [4096], P('store')
- cluster_grad: float32 [1024, 2], P('store')
- first_proj_grad: float32 [1024, 256], P('store')
- second_proj_grad: float32 [1024, 64], P('store')
- head_grad: float32 [1024, 2560], P(None, 'store')
- first_tail_grad: float32 [256, 5120], P(None, 'store')
- second_tail_grad: float32 [64, 26624], P(None, 'store')
The draws below stay inside these ranges and needn't reach their ends.
Inputs may be any that keep to these rules, and one draw needn't show every extreme that they name: `lengths`: some sequence has exactly 128 tokens in every draw. `near_slots`: the 16 candidates of one token at one owner are distinct.
All inputs are finite; a program needn't handle non-finite values.
Results may differ from the reference program's by a relative error of at most 0.025.
Values may be sent and summed in bfloat16 or wider, within the bound.
No kernel may reach another device: no remote copies, remote signals or barrier semaphores. Data moves between devices by JAX's collectives and lax.ppermute only.
A program may use at most 320 MiB of HBM per device.

```python
import math
import jax
import jax.numpy as jnp
from jax import lax

D = 1024
HEADS = 16
HD = 64
FF = 4096
P1D = 256
P2D = 64
T1_DEV = 640
T2_DEV = 3328
TOK_DEV = 128
DS_DEV = 4096
NB = 128
KB = 16
K = 128
HEAD = 2560
V1 = 5120
V2 = 26624
VOCAB = 34304
NSEQ = 32
TOKENS = 4096
STORE_ROWS = 32768
N_DP = 4
N_STORE = 8


store_word_cap = 32704


def draw_lengths(key, part):
    base_len = jax.random.randint(jax.random.fold_in(key, 1), (NSEQ,), TOK_DEV // 2, TOK_DEV + 1)
    chosen_seq = jax.random.randint(jax.random.fold_in(key, 2), (), 0, NSEQ)
    return jnp.where(jnp.arange(NSEQ) == chosen_seq, TOK_DEV, base_len).astype(jnp.int32)


def word_draw(key):
    base_key = jax.random.fold_in(key, 17)
    branch = jax.random.randint(jax.random.fold_in(base_key, 1), (TOKENS,), 0, 2)
    common = jax.random.randint(jax.random.fold_in(base_key, 2), (TOKENS,), 0, 64)
    spread = jax.random.randint(jax.random.fold_in(base_key, 3), (TOKENS,), 0, VOCAB)
    return jnp.where(branch == 0, common, spread).astype(jnp.int32)


def draw_targets(key, part):
    return word_draw(key)


def draw_near_words(key, part):
    own_words = word_draw(key)
    word_limit = min(VOCAB, store_word_cap)
    base_key = jax.random.fold_in(key, 29)
    hit_rate = jax.random.randint(jax.random.fold_in(base_key, 1), (TOKENS, 1), 0, 9)
    rolled = jax.random.randint(jax.random.fold_in(base_key, 2), (TOKENS, K), 0, 16)
    others = jax.random.randint(jax.random.fold_in(base_key, 3), (TOKENS, K), 0, word_limit)
    hits = (rolled < hit_rate) & (own_words[:, None] < word_limit)
    return jnp.where(hits, own_words[:, None], others).astype(jnp.int32)


def draw_near_slots(key, part):
    shape_base = (N_DP, N_STORE, TOK_DEV, N_STORE, 1)
    start_slot = jax.random.randint(jax.random.fold_in(key, 41), shape_base, 0, NB)
    stride = 2 * jax.random.randint(jax.random.fold_in(key, 42), shape_base, 0, NB // 2) + 1
    return ((start_slot + stride * jnp.arange(KB)) % NB).astype(jnp.int32)


def with_ends(array, stream_key, least, largest):
    place = [jax.random.randint(jax.random.fold_in(stream_key, axis), (), 0, length) for axis, length in enumerate(array.shape)]
    widest = array.shape.index(max(array.shape))
    next_to = place[:widest] + [(place[widest] + 1) % array.shape[widest]] + place[widest + 1:]
    return array.at[tuple(place)].set(least).at[tuple(next_to)].set(largest)


def steps_of(rng, shape, cuts, smallest, high):
    def one(position, parts):
        heights = jax.random.uniform(jax.random.fold_in(jax.random.fold_in(rng, 6), position), (parts,), jnp.float32, smallest / len(cuts), high / len(cuts))
        return jnp.repeat(jnp.exp(heights), shape[position] // parts).reshape((-1,) + (1,) * (len(shape) - position - 1))

    loudness = one(*cuts[0])
    for cut in cuts[1:]:
        loudness = loudness * one(*cut)
    return loudness


def normal_values(own_key, dims, deviation, reach, cuts=(), held_as=jnp.bfloat16):
    level = steps_of(own_key, dims, cuts, -0.22, 0.18) if cuts else 1.0
    values = jax.random.normal(own_key, dims, jnp.float32) * deviation * level
    return jnp.minimum(jnp.maximum(values, -reach), reach).astype(held_as)


def setup_inputs(seed: int = 0) -> dict:
    key_list = jax.random.split(jax.random.key(seed), 22)
    inputs = normal_values(key_list[0], (TOKENS, D), 1.0, 6.0, ((0, 32),))
    lengths = draw_lengths(jax.random.fold_in(key_list[21], 71), 0)
    targets = draw_targets(jax.random.fold_in(key_list[21], 71), 0)
    attn_qkv = normal_values(key_list[3], (3, D, D), D ** -0.5, 0.1875)
    attn_out = normal_values(key_list[4], (D, D), (D // 32) ** -0.5, 1.0)
    ffn_up = normal_values(key_list[5], (D, FF), D ** -0.5, 0.1875)
    ffn_down = normal_values(key_list[6], (FF, D), FF ** -0.5, 0.09375)
    norm_gains = jnp.clip(1.0 + 0.15 * jax.random.normal(key_list[7], (3, D), jnp.float32), 0.25, 1.75)
    norm_shifts = normal_values(key_list[8], (3, D), 0.3, 1.5, (), jnp.float32)
    biases = normal_values(key_list[9], (4, D), 0.3, 1.5, (), jnp.float32)
    up_bias = normal_values(key_list[10], (FF,), 0.3, 1.5, (), jnp.float32)
    cluster_proj = normal_values(key_list[11], (D, 2), D ** -0.5, 0.1875)
    proj_first = normal_values(key_list[12], (D, P1D), D ** -0.5, 0.1875)
    proj_second = normal_values(key_list[13], (D, P2D), D ** -0.5, 0.1875)
    head_words = normal_values(key_list[14], (D, HEAD), D ** -0.5, 0.1875, ((1, 8),))
    tail_first = normal_values(key_list[15], (P1D, V1), P1D ** -0.5, 0.375, ((1, 8),))
    tail_second = normal_values(key_list[16], (P2D, V2), P2D ** -0.5, 0.75, ((1, 8),))
    store_keys = normal_values(key_list[17], (STORE_ROWS, D), 1.0, 6.0, ((0, 8),))
    block_rows = with_ends(jax.random.randint(key_list[18], (N_DP, N_STORE, N_STORE, NB), 0, DS_DEV), jax.random.fold_in(key_list[18], 1), 0, DS_DEV - 1).astype(jnp.int32)
    near_slots = draw_near_slots(jax.random.fold_in(key_list[21], 71), 0)
    near_words = draw_near_words(jax.random.fold_in(key_list[21], 71), 0)
    return dict(inputs=inputs, lengths=lengths, targets=targets, attn_qkv=attn_qkv, attn_out=attn_out, ffn_up=ffn_up, ffn_down=ffn_down, norm_gains=norm_gains, norm_shifts=norm_shifts, biases=biases, up_bias=up_bias, cluster_proj=cluster_proj, proj_first=proj_first, proj_second=proj_second, head_words=head_words, tail_first=tail_first, tail_second=tail_second, store_keys=store_keys, block_rows=block_rows, near_slots=near_slots, near_words=near_words)


@jax.custom_vjp
def low(v):
    return lax.optimization_barrier(v.astype(jnp.bfloat16)).astype(jnp.float32)

@jax.custom_vjp
def low_back(v):
    return v

def low_keep(v):
    return (low(v), None)

def low_pass(kept, grad):
    return (grad,)

def back_keep(v):
    return (v, None)

def back_low(kept, grad):
    return (low(grad),)
low.defvjp(low_keep, low_pass)
low_back.defvjp(back_keep, back_low)
EPS = 1e-05
NEAR_WEIGHT = 0.25
NEG_FILL = -1e+30
HIGH = lax.Precision.HIGHEST

def layer_norm(values, gain_row, shift_row):
    row_mean = lax.optimization_barrier(jnp.mean(values, axis=-1, keepdims=True))
    centred = values - row_mean
    variance = lax.optimization_barrier(jnp.mean(centred * centred, axis=-1, keepdims=True))
    return centred * lax.rsqrt(variance + EPS) * gain_row + shift_row

def matmul(left, right):
    return jnp.dot(left, right, precision=HIGH)

def pick_column(logits, where_col):
    columns = jnp.arange(logits.shape[1])
    return lax.optimization_barrier(jnp.sum(jnp.where(columns[None, :] == where_col[:, None], logits, 0.0), axis=1))

def sequence_loss(weights, seq_in, seq_inputs, store_keys, key_norms):
    attn_qkv, attn_out, ffn_up, ffn_down, norm_gains, norm_shifts, biases, up_bias, cluster_proj, proj_first, proj_second, head_words, tail_first, tail_second = weights
    length, target_seq, near_seq, row_ids, slot_ids = seq_inputs
    positions = jnp.arange(TOK_DEV)
    valid_mask = (positions < length).astype(jnp.float32)
    allowed = (positions[None, :] <= positions[:, None]) & (positions[None, :] < length)
    normed = low(layer_norm(seq_in, norm_gains[0], norm_shifts[0]))
    query_rows = low(low_back(matmul(normed, attn_qkv[0]) + biases[0])).reshape(TOK_DEV, HEADS, HD)
    key_rows = low(low_back(matmul(normed, attn_qkv[1]))).reshape(TOK_DEV, HEADS, HD)
    valued = low(low_back(matmul(normed, attn_qkv[2]) + biases[1])).reshape(TOK_DEV, HEADS, HD)
    scores = jnp.einsum('thd,shd->hts', query_rows, key_rows, precision=HIGH) * HD ** (-0.5)
    scores = low_back(jnp.where(allowed[None], scores, NEG_FILL))
    attn_probs = jax.nn.softmax(scores, axis=-1)
    mixed_rows = jnp.einsum('hts,shd->thd', low(attn_probs), valued, precision=HIGH).reshape(TOK_DEV, D)
    mixed_rows = low(low_back(mixed_rows))
    first_sum = seq_in + low_back(matmul(mixed_rows, attn_out) + biases[2])
    second_in = low(layer_norm(first_sum, norm_gains[1], norm_shifts[1]))
    pre_act = low_back(matmul(second_in, ffn_up) + up_bias)
    activation = low(jnp.maximum(pre_act, 0.0))
    second_sum = first_sum + low_back(matmul(activation, ffn_down) + biases[3])
    hidden = low(layer_norm(second_sum, norm_gains[2], norm_shifts[2]))
    cluster = matmul(hidden, cluster_proj)
    tail_in_one = low(matmul(hidden, proj_first))
    tail_in_two = low(matmul(hidden, proj_second))
    head_logits = low_back(matmul(hidden, head_words))
    one_copies = low_back(jnp.broadcast_to(tail_in_one[:, None, :], (TOK_DEV, N_STORE, P1D)))
    two_copies = low_back(jnp.broadcast_to(tail_in_two[:, None, :], (TOK_DEV, N_STORE, P2D)))
    first_logits = low_back(jnp.einsum('tnk,knv->tnv', one_copies, tail_first.reshape(P1D, N_STORE, T1_DEV), precision=HIGH)).reshape(TOK_DEV, V1)
    second_logits = low_back(jnp.einsum('tnk,knv->tnv', two_copies, tail_second.reshape(P2D, N_STORE, T2_DEV), precision=HIGH)).reshape(TOK_DEV, V2)
    in_first = ((target_seq >= HEAD) & (target_seq < HEAD + V1)).astype(jnp.float32)
    in_second = (target_seq >= HEAD + V1).astype(jnp.float32)
    picked = pick_column(head_logits, target_seq) + pick_column(first_logits, target_seq - HEAD) + pick_column(second_logits, target_seq - HEAD - V1)
    log_head = jnp.log(lax.optimization_barrier(jnp.sum(jnp.exp(head_logits), axis=1)) + lax.optimization_barrier(jnp.sum(jnp.exp(cluster), axis=1)))
    log_first = jnp.log(lax.optimization_barrier(jnp.sum(jnp.exp(first_logits), axis=1)))
    log_second = jnp.log(lax.optimization_barrier(jnp.sum(jnp.exp(second_logits), axis=1)))
    log_model = picked - log_head + in_first * (cluster[:, 0] - log_first) + in_second * (cluster[:, 1] - log_second)
    block_keys = store_keys[row_ids].astype(jnp.float32)
    block_norms = key_norms[row_ids]
    key_scale = 1.0 / math.sqrt(D)
    dense_dots = jnp.einsum('td,nbd->tnb', hidden, block_keys, precision=HIGH)
    scaled = dense_dots * key_scale - block_norms[None] * (0.5 * key_scale)
    chosen = low_back(jnp.take_along_axis(scaled, slot_ids, axis=2).reshape(TOK_DEV, K))
    near_probs = jax.nn.softmax(chosen, axis=1)
    matched = (near_seq == target_seq[:, None]).astype(jnp.float32)
    near_mass = lax.optimization_barrier(jnp.sum(near_probs * matched, axis=1))
    mixture = NEAR_WEIGHT * near_mass + (1.0 - NEAR_WEIGHT) * jnp.exp(log_model)
    return -valid_mask * jnp.log(mixture)

def reference(inputs, lengths, targets, attn_qkv, attn_out, ffn_up, ffn_down, norm_gains, norm_shifts, biases, up_bias, cluster_proj, proj_first, proj_second, head_words, tail_first, tail_second, store_keys, block_rows, near_slots, near_words):
    weights = tuple((weight.astype(jnp.float32) for weight in (attn_qkv, attn_out, ffn_up, ffn_down, norm_gains, norm_shifts, biases, up_bias, cluster_proj, proj_first, proj_second, head_words, tail_first, tail_second)))
    seq_block = inputs.astype(jnp.float32).reshape(NSEQ, TOK_DEV, D)
    offsets = (jnp.arange(N_STORE) * DS_DEV).astype(jnp.int32)
    row_ids = block_rows.transpose(0, 2, 1, 3).reshape(NSEQ, N_STORE, NB).astype(jnp.int32) + offsets[None, :, None]
    slot_ids = near_slots.transpose(0, 3, 2, 1, 4).reshape(NSEQ, TOK_DEV, N_STORE, KB).astype(jnp.int32)
    seq_inputs = (lengths, targets.reshape(NSEQ, TOK_DEV), near_words.reshape(NSEQ, TOK_DEV, K), row_ids, slot_ids)
    key_norms = lax.optimization_barrier(jnp.sum(jnp.square(store_keys.astype(jnp.float32)), axis=1))

    def objective(weight_set, seq_all):

        def per_sequence(seq_item):
            seq_in, seq_data = seq_item
            return sequence_loss(weight_set, seq_in, seq_data, store_keys, key_norms)
        losses = lax.map(jax.checkpoint(per_sequence), (seq_all, seq_inputs))
        return (jnp.sum(losses), losses)
    summed, pull_back, losses = jax.vjp(objective, weights, seq_block, has_aux=True)
    weight_grads, seq_grads = pull_back(jnp.ones_like(summed))
    return (losses.reshape(TOKENS), seq_grads.reshape(TOKENS, D), weight_grads[0], weight_grads[1], weight_grads[2], weight_grads[3], weight_grads[4], weight_grads[5], weight_grads[6], weight_grads[7], weight_grads[8], weight_grads[9], weight_grads[10], weight_grads[11], weight_grads[12], weight_grads[13])
```

```python
import math

import jax
import jax.numpy as jnp
from jax import lax
from jax.sharding import PartitionSpec as P

HEADS = 16
HD = 64


EPS = 1e-05
NEAR_WEIGHT = 0.25
NEG_FILL = -1e30
SPAN_SOURCES = 8


def product(left, right):
    return jnp.dot(left, right, preferred_element_type=jnp.float32)


def norm_forward(values, gain_row, shift_row):
    row_mean = jnp.mean(values, axis=-1, keepdims=True)
    centred = values - row_mean
    inverse = lax.rsqrt(jnp.mean(centred * centred, axis=-1, keepdims=True) + EPS)
    unit_rows = centred * inverse
    return (unit_rows * gain_row + shift_row, unit_rows, inverse)


def norm_backward(grad_out, unit_rows, inverse, gain_row):
    scaled = grad_out * gain_row
    grad_in = inverse * (
        scaled
        - jnp.mean(scaled, axis=-1, keepdims=True)
        - unit_rows * jnp.mean(scaled * unit_rows, axis=-1, keepdims=True)
    )
    return (grad_in, jnp.sum(grad_out * unit_rows, axis=0), jnp.sum(grad_out, axis=0))


def attention_scores(query_low, key_low, allowed):
    scores = jnp.einsum(
        "thd,shd->hts", query_low, key_low, preferred_element_type=jnp.float32
    ) * HD ** (-0.5)
    return jnp.where(allowed[None], scores, NEG_FILL)


def pick_column(logits, where_col):
    columns = jnp.arange(logits.shape[1])
    return jnp.sum(jnp.where(columns[None, :] == where_col[:, None], logits, 0.0), axis=1)


def one_hot(logits, where_col):
    columns = jnp.arange(logits.shape[1])
    return (columns[None, :] == where_col[:, None]).astype(jnp.float32)


def dp_partner(step):
    count = lax.axis_size("dp")
    mine = lax.axis_index("dp")
    if count & (count - 1) == 0:
        pairs = [(s, s ^ step) for s in range(count)]
        return pairs, mine ^ step
    return [(s, (s + step) % count) for s in range(count)], (mine + step) % count


def dp_gather(rows):
    parts = [rows]
    for step in range(1, lax.axis_size("dp")):
        parts.append(lax.ppermute(rows, "dp", dp_partner(step)[0]))
    return jnp.concatenate(parts, axis=0)


def dp_columns(*arrays):
    count = lax.axis_size("dp")

    def block_of(index):
        return jnp.concatenate(
            [
                lax.dynamic_slice_in_dim(a, index * (a.shape[1] // count), a.shape[1] // count, 1)
                for a in arrays
            ],
            axis=1,
        )

    parts = [block_of(lax.axis_index("dp"))]
    for step in range(1, count):
        pairs, target = dp_partner(step)
        parts.append(lax.ppermute(block_of(target), "dp", pairs))
    return jnp.concatenate(parts, axis=0)


def transposed_product(left, right):
    return lax.dot_general(
        left, right, (((0,), (0,)), ((), ())), preferred_element_type=jnp.float32
    )


def shards(
    inputs,
    lengths,
    targets,
    attn_qkv,
    attn_out,
    ffn_up,
    ffn_down,
    norm_gains,
    norm_shifts,
    biases,
    up_bias,
    cluster_proj,
    proj_first,
    proj_second,
    head_words,
    tail_first,
    tail_second,
    store_keys,
    block_rows,
    near_slots,
    near_words,
):
    tokens_here = inputs.shape[0]
    d_model = inputs.shape[1]
    sources = lax.axis_size("store")
    dp_count = lax.axis_size("dp")
    my_index = lax.axis_index("store")
    group_rows = tokens_here * sources
    head_cols = head_words.shape[1]
    first_cols = tail_first.shape[1]
    second_cols = tail_second.shape[1]
    head_total = head_cols * sources
    first_total = first_cols * sources
    slots_each = near_slots.shape[-1]
    candidates = block_rows.shape[-1]
    key_scale = 1.0 / math.sqrt(d_model)
    positions = jnp.arange(tokens_here)
    length_now = lengths[0]
    valid_mask = (positions < length_now).astype(jnp.int32)
    allowed = (positions[None, :] <= positions[:, None]) & (positions[None, :] < length_now)

    word_rows = near_words.T.reshape(sources, slots_each, tokens_here)
    valid_rows = jnp.broadcast_to(valid_mask[None, None, :], (sources, 1, tokens_here))
    sent = jnp.concatenate([word_rows, valid_rows], axis=1)
    got = lax.all_to_all(sent, "store", split_axis=0, concat_axis=0, tiled=True)
    group_words = got[:, :slots_each, :]
    group_valid = got[:, slots_each, :].reshape(group_rows).astype(jnp.float32)
    target_rows = targets.reshape(sources, 1, tokens_here)
    slot_rows = jnp.transpose(near_slots[0, 0], (1, 2, 0))
    weight_rows = 1.0 + (group_words == target_rows).astype(jnp.float32)
    which = jnp.arange(candidates)[None, :, None]
    code = jnp.zeros((sources, candidates, tokens_here), jnp.float32)
    for m in range(slots_each):
        code = jnp.where(slot_rows[:, m : m + 1, :] == which, weight_rows[:, m : m + 1, :], code)
    key_block = jnp.take(store_keys, block_rows[0, 0], axis=0)
    key_wide = key_block.astype(jnp.float32)
    norm_block = jnp.sum(key_wide * key_wide, axis=2)

    block_in = inputs.astype(jnp.float32)
    normed, unit_one, inv_one = norm_forward(block_in, norm_gains[0], norm_shifts[0])
    normed_low = normed.astype(jnp.bfloat16)
    projected = jnp.einsum("td,cde->cte", normed_low, attn_qkv, preferred_element_type=jnp.float32)
    query_low = (projected[0] + biases[0]).astype(jnp.bfloat16).reshape(tokens_here, HEADS, HD)
    key_low = projected[1].astype(jnp.bfloat16).reshape(tokens_here, HEADS, HD)
    value_low = (projected[2] + biases[1]).astype(jnp.bfloat16).reshape(tokens_here, HEADS, HD)
    scores = attention_scores(query_low, key_low, allowed)
    top_score = jnp.max(scores, axis=-1, keepdims=True)
    log_total = top_score + jnp.log(jnp.sum(jnp.exp(scores - top_score), axis=-1, keepdims=True))
    attn_probs = jnp.exp(scores - log_total)
    mixed_low = (
        jnp.einsum(
            "hts,shd->thd",
            attn_probs.astype(jnp.bfloat16),
            value_low,
            preferred_element_type=jnp.float32,
        )
        .reshape(tokens_here, d_model)
        .astype(jnp.bfloat16)
    )
    first_sum = block_in + product(mixed_low, attn_out) + biases[2]
    second_norm, unit_two, inv_two = norm_forward(first_sum, norm_gains[1], norm_shifts[1])
    second_low = second_norm.astype(jnp.bfloat16)
    pre_act = product(second_low, ffn_up) + up_bias
    act_low = jnp.maximum(pre_act, 0.0).astype(jnp.bfloat16)
    second_sum = first_sum + product(act_low, ffn_down) + biases[3]
    final_norm, unit_three, inv_three = norm_forward(second_sum, norm_gains[2], norm_shifts[2])
    hidden_low = final_norm.astype(jnp.bfloat16)

    normed_all = dp_gather(normed_low)
    mixed_all = dp_gather(mixed_low)
    second_all = dp_gather(second_low)
    act_all = dp_gather(act_low)

    rows_all = lax.all_gather(hidden_low, "store", axis=0, tiled=True)
    dense_dots = jnp.einsum(
        "jnd,jtd->jnt",
        key_block,
        rows_all.reshape(sources, tokens_here, d_model),
        preferred_element_type=jnp.float32,
    )
    scored = dense_dots * key_scale - norm_block[:, :, None] * (0.5 * key_scale)
    member = code > 0.5
    near_top = jnp.max(jnp.where(member, scored, NEG_FILL), axis=1)
    near_exp = jnp.where(member, jnp.exp(scored - near_top[:, None, :]), 0.0)
    near_sum = jnp.sum(near_exp, axis=1)
    near_hit = jnp.sum(jnp.where(code > 1.5, near_exp, 0.0), axis=1)

    span_sources = min(SPAN_SOURCES, sources)
    span_rows = span_sources * tokens_here
    span_count = sources // span_sources

    def span_inputs(span_index):
        start = span_index * span_rows
        if span_count == 1:
            rows_here, words_here = rows_all, targets
        else:
            rows_here = lax.dynamic_slice_in_dim(rows_all, start, span_rows, 0)
            words_here = lax.dynamic_slice_in_dim(targets, start, span_rows, 0)
        ones_here = product(rows_here, proj_first).astype(jnp.bfloat16)
        twos_here = product(rows_here, proj_second).astype(jnp.bfloat16)
        head_pos = words_here - my_index * head_cols
        first_pos = words_here - head_total - my_index * first_cols
        second_pos = words_here - head_total - first_total - my_index * second_cols
        return (rows_here, ones_here, twos_here, words_here, head_pos, first_pos, second_pos)

    def word_stats(span_index):
        rows_here, ones_here, twos_here, words_here, head_pos, first_pos, second_pos = span_inputs(
            span_index
        )
        head_logits = product(rows_here, head_words)
        first_logits = product(ones_here, tail_first)
        second_logits = product(twos_here, tail_second)
        picked = (
            pick_column(head_logits, head_pos)
            + pick_column(first_logits, first_pos)
            + pick_column(second_logits, second_pos)
        )
        return jnp.stack(
            [
                jnp.sum(jnp.exp(head_logits), axis=1),
                jnp.sum(jnp.exp(first_logits), axis=1),
                jnp.sum(jnp.exp(second_logits), axis=1),
                picked,
            ]
        )

    if span_count == 1:
        row_stats = word_stats(0)
    else:
        row_stats = lax.map(word_stats, jnp.arange(span_count))
        row_stats = jnp.moveaxis(row_stats, 1, 0).reshape(4, group_rows)
    near_stats = jnp.stack([near_top, near_sum, near_hit]).reshape(3, group_rows)
    all_stats = lax.all_gather(jnp.concatenate([row_stats, near_stats]), "store", axis=0)

    cluster_logits = lax.dot_general(
        cluster_proj, rows_all, (((0,), (1,)), ((), ())), preferred_element_type=jnp.float32
    )
    in_first = ((targets >= head_total) & (targets < head_total + first_total)).astype(jnp.float32)
    in_second = (targets >= head_total + first_total).astype(jnp.float32)
    word_sums = jnp.sum(all_stats[:, :4], axis=0)
    log_head = jnp.log(word_sums[0] + jnp.exp(cluster_logits[0]) + jnp.exp(cluster_logits[1]))
    log_first = jnp.log(word_sums[1])
    log_second = jnp.log(word_sums[2])
    log_model = (
        word_sums[3]
        - log_head
        + in_first * (cluster_logits[0] - log_first)
        + in_second * (cluster_logits[1] - log_second)
    )
    top_all = jnp.max(all_stats[:, 4], axis=0)
    shrink = jnp.exp(all_stats[:, 4] - top_all[None, :])
    near_total = jnp.sum(shrink * all_stats[:, 5], axis=0)
    near_mass = jnp.sum(shrink * all_stats[:, 6], axis=0) / near_total
    model_prob = jnp.exp(log_model)
    mixture = NEAR_WEIGHT * near_mass + (1.0 - NEAR_WEIGHT) * model_prob
    loss_all = -group_valid * jnp.log(mixture)
    model_weight = group_valid * (1.0 - NEAR_WEIGHT) * model_prob / mixture
    near_weight = group_valid * NEAR_WEIGHT / mixture
    own_shrink = jnp.exp(near_top.reshape(group_rows) - top_all) / near_total
    prob_rows = (near_weight * own_shrink).reshape(sources, 1, tokens_here)
    mass_rows = near_mass.reshape(sources, 1, tokens_here)
    dense_grad = (-prob_rows * near_exp * ((code - 1.0) - mass_rows)).astype(jnp.bfloat16)
    near_term = (
        jnp.einsum("jnt,jnd->jtd", dense_grad, key_block, preferred_element_type=jnp.float32)
        * key_scale
    ).reshape(group_rows, d_model)

    def word_grads(span_index):
        rows_here, ones_here, twos_here, words_here, head_pos, first_pos, second_pos = span_inputs(
            span_index
        )
        start = span_index * span_rows

        def part(values):
            if span_count == 1:
                return values
            return lax.dynamic_slice_in_dim(values, start, span_rows, 0)

        weight_here = part(model_weight)
        head_logits = product(rows_here, head_words)
        first_logits = product(ones_here, tail_first)
        second_logits = product(twos_here, tail_second)
        head_grad = (
            weight_here[:, None]
            * (jnp.exp(head_logits - part(log_head)[:, None]) - one_hot(head_logits, head_pos))
        ).astype(jnp.bfloat16)
        first_grad = (
            (weight_here * part(in_first))[:, None]
            * (jnp.exp(first_logits - part(log_first)[:, None]) - one_hot(first_logits, first_pos))
        ).astype(jnp.bfloat16)
        second_grad = (
            (weight_here * part(in_second))[:, None]
            * (
                jnp.exp(second_logits - part(log_second)[:, None])
                - one_hot(second_logits, second_pos)
            )
        ).astype(jnp.bfloat16)
        back_one = product(first_grad, tail_first.T).astype(jnp.bfloat16)
        back_two = product(second_grad, tail_second.T).astype(jnp.bfloat16)
        row_term = (
            product(head_grad, head_words.T)
            + product(back_one, proj_first.T)
            + product(back_two, proj_second.T)
            + part(near_term)
        ).astype(jnp.bfloat16)
        return (
            row_term,
            transposed_product(rows_here, head_grad),
            transposed_product(ones_here, first_grad),
            transposed_product(twos_here, second_grad),
            transposed_product(rows_here, back_one),
            transposed_product(rows_here, back_two),
        )

    if span_count == 1:
        row_terms, head_acc, first_acc, second_acc, pone_acc, ptwo_acc = word_grads(0)
    else:

        def span_step(carry, span_index):
            row_term, *terms = word_grads(span_index)
            return (tuple(a + b for a, b in zip(carry, terms)), row_term)

        start_acc = tuple(
            jnp.zeros(w.shape, jnp.float32)
            for w in (head_words, tail_first, tail_second, proj_first, proj_second)
        )
        (head_acc, first_acc, second_acc, pone_acc, ptwo_acc), row_terms = lax.scan(
            span_step, start_acc, jnp.arange(span_count)
        )
        row_terms = row_terms.reshape(group_rows, d_model)
    row_back = lax.psum_scatter(row_terms, "store", scatter_dimension=0, tiled=True)

    def own(values):
        return lax.dynamic_slice_in_dim(values, my_index * tokens_here, tokens_here, 0)

    token_loss = own(loss_all)
    cluster_zero = own(model_weight * (jnp.exp(cluster_logits[0] - log_head) - in_first))
    cluster_one = own(model_weight * (jnp.exp(cluster_logits[1] - log_head) - in_second))
    cluster_wide = cluster_proj.astype(jnp.float32)
    hidden_grad = (
        row_back.astype(jnp.float32)
        + cluster_zero[:, None] * cluster_wide[:, 0][None, :]
        + cluster_one[:, None] * cluster_wide[:, 1][None, :]
    )
    cluster_rows = jnp.stack([cluster_zero, cluster_one]).astype(jnp.bfloat16)
    cluster_acc = product(cluster_rows, hidden_low)
    second_grad, gain_three, shift_three = norm_backward(
        hidden_grad, unit_three, inv_three, norm_gains[2]
    )
    down_in = second_grad.astype(jnp.bfloat16)
    bias_down = jnp.sum(down_in.astype(jnp.float32), axis=0)
    down_part = transposed_product(act_all, dp_columns(down_in)).astype(jnp.bfloat16)
    act_grad = product(down_in, ffn_down.T)
    pre_grad = jnp.where(pre_act > 0, act_grad, 0.0).astype(jnp.bfloat16)
    up_bias_acc = jnp.sum(pre_grad.astype(jnp.float32), axis=0)
    up_part = transposed_product(second_all, dp_columns(pre_grad)).astype(jnp.bfloat16)
    norm_two_grad = product(pre_grad, ffn_up.T)
    back_second, gain_two, shift_two = norm_backward(
        norm_two_grad, unit_two, inv_two, norm_gains[1]
    )
    first_grad_sum = second_grad + back_second
    attn_in = first_grad_sum.astype(jnp.bfloat16)
    bias_attn = jnp.sum(attn_in.astype(jnp.float32), axis=0)
    out_part = transposed_product(mixed_all, dp_columns(attn_in)).astype(jnp.bfloat16)
    mixed_grad = product(attn_in, attn_out.T).astype(jnp.bfloat16).reshape(tokens_here, HEADS, HD)
    prob_grad = jnp.einsum(
        "thd,shd->hts", mixed_grad, value_low, preferred_element_type=jnp.float32
    )
    row_delta = jnp.sum(attn_probs * prob_grad, axis=-1, keepdims=True)
    attn_score_grad = (attn_probs * (prob_grad - row_delta)).astype(jnp.bfloat16)
    query_grad = (
        jnp.einsum("hts,shd->thd", attn_score_grad, key_low, preferred_element_type=jnp.float32)
        * HD ** (-0.5)
    ).astype(jnp.bfloat16).reshape(tokens_here, d_model)
    key_grad = (
        jnp.einsum("hts,thd->shd", attn_score_grad, query_low, preferred_element_type=jnp.float32)
        * HD ** (-0.5)
    ).astype(jnp.bfloat16).reshape(tokens_here, d_model)
    value_grad = jnp.einsum(
        "hts,thd->shd",
        attn_probs.astype(jnp.bfloat16),
        mixed_grad,
        preferred_element_type=jnp.float32,
    ).astype(jnp.bfloat16).reshape(tokens_here, d_model)
    qkv_part = transposed_product(
        normed_all, dp_columns(query_grad, key_grad, value_grad)
    ).astype(jnp.bfloat16)
    normed_grad = (
        lax.dot_general(
            query_grad, attn_qkv[0], (((1,), (1,)), ((), ())), preferred_element_type=jnp.float32
        )
        + lax.dot_general(
            key_grad, attn_qkv[1], (((1,), (1,)), ((), ())), preferred_element_type=jnp.float32
        )
        + lax.dot_general(
            value_grad, attn_qkv[2], (((1,), (1,)), ((), ())), preferred_element_type=jnp.float32
        )
    )
    back_first, gain_one, shift_one = norm_backward(normed_grad, unit_one, inv_one, norm_gains[0])
    input_grad = first_grad_sum + back_first

    vocab_low = tuple(
        a.astype(jnp.bfloat16) for a in (head_acc, first_acc, second_acc, pone_acc, ptwo_acc)
    )
    head_low, first_low, second_low_sum, pone_low, ptwo_low = lax.psum(vocab_low, "dp")

    upb_rows = up_bias_acc.reshape(sources, -1, d_model // sources)
    upb_rows = jnp.transpose(upb_rows, (1, 0, 2)).reshape(-1, d_model)
    small = jnp.concatenate(
        [
            jnp.stack([gain_one, gain_two, gain_three, shift_one, shift_two, shift_three]),
            jnp.stack(
                [
                    jnp.sum(query_grad.astype(jnp.float32), axis=0),
                    jnp.sum(value_grad.astype(jnp.float32), axis=0),
                    bias_attn,
                    bias_down,
                ]
            ),
            cluster_acc,
            upb_rows,
        ]
    )
    small_rows = small.shape[0]
    down_here = lax.psum_scatter(down_part, "store", scatter_dimension=0, tiled=True)
    up_here = lax.psum_scatter(up_part, "store", scatter_dimension=0, tiled=True)
    packed = jnp.concatenate(
        [qkv_part, out_part, pone_low, ptwo_low, small.T.astype(jnp.bfloat16)], axis=1
    )
    packed_here = lax.psum_scatter(packed, "store", scatter_dimension=0, tiled=True)
    down_out = lax.all_gather(down_here, "dp", axis=1, tiled=True).astype(jnp.float32)
    up_out = lax.all_gather(up_here, "dp", axis=1, tiled=True).astype(jnp.float32)
    block = d_model // dp_count
    wide = 4 * block
    d_here = d_model // sources
    proj_cols = proj_first.shape[1] + proj_second.shape[1]
    pone_out = packed_here[:, wide : wide + proj_first.shape[1]].astype(jnp.float32)
    ptwo_out = packed_here[:, wide + proj_first.shape[1] : wide + proj_cols].astype(jnp.float32)
    travel = jnp.concatenate([packed_here[:, :wide], packed_here[:, wide + proj_cols :]], axis=1)
    packed_all = lax.all_gather(travel, "dp", axis=0)
    parts = packed_all[:, :, :wide].reshape(dp_count, d_here, 4, block)
    parts = jnp.transpose(parts, (2, 1, 0, 3)).reshape(4, d_here, d_model).astype(jnp.float32)
    qkv_out = parts[:3]
    out_out = parts[3]
    small_sum = jnp.sum(packed_all[:, :, wide:].astype(jnp.float32), axis=0).T
    gains_out = small_sum[:3]
    shifts_out = small_sum[3:6]
    biases_out = small_sum[6:10]
    cluster_out = small_sum[10:12].T
    upb_out = small_sum[12:small_rows].reshape(-1)
    return (
        token_loss,
        input_grad,
        qkv_out,
        out_out,
        up_out,
        down_out,
        gains_out,
        shifts_out,
        biases_out,
        upb_out,
        cluster_out,
        pone_out,
        ptwo_out,
        head_low.astype(jnp.float32),
        first_low.astype(jnp.float32),
        second_low_sum.astype(jnp.float32),
    )


def solution(mesh):
    return jax.shard_map(
        shards,
        mesh=mesh,
        in_specs=(
            P(("dp", "store"), None),
            P(("dp", "store")),
            P("dp"),
            P(),
            P(),
            P(),
            P(),
            P(),
            P(),
            P(),
            P(),
            P(),
            P(),
            P(),
            P(None, "store"),
            P(None, "store"),
            P(None, "store"),
            P("store", None),
            P("dp", "store", None, None),
            P("dp", "store", None, None, None),
            P(("dp", "store"), None),
        ),
        out_specs=(
            P(("dp", "store")),
            P(("dp", "store"), None),
            P(None, "store", None),
            P("store", None),
            P("store", None),
            P("store", None),
            P(None, "store"),
            P(None, "store"),
            P(None, "store"),
            P("store"),
            P("store", None),
            P("store", None),
            P("store", None),
            P(None, "store"),
            P(None, "store"),
            P(None, "store"),
        ),
        check_vma=False,
    )
```
